32 devices in a mesh: grp: 2 (over x), tok: 16 (over z, y, core).
Axes of the slice: x: 2, y: 2, z: 4, core: 2. Of those that a mesh axis runs over, the one named last changes fastest.
Arguments:
- keys: bfloat16 [4096, 1024], P(('grp', 'tok')), parts along dimension 0, may hold values from -6 to 6
- values: bfloat16 [4096, 1024], P(('grp', 'tok')), parts along dimension 0, may hold values from -6 to 6
- queries: bfloat16 [4096, 1024], P(('grp', 'tok')), parts along dimension 0, may hold values from -6 to 6
- rates: float32 [2, 4096], P(None, ('grp', 'tok')), parts along dimension 1, may hold values from 0.3 to 3
- fast_weights: bfloat16 [2, 3, 512, 512], replicated, may hold values from -0.25 to 0.25
Outputs:
- readout: bfloat16 [4096, 1024], P(('grp', 'tok')), parts along dimension 0
- new_weights: bfloat16 [4, 3, 512, 512], P('grp'), parts along dimension 0
The draws below stay inside these ranges and needn't reach their ends.
There are 2 independent parts, one for each index of `grp`. The reference program is written for one: setup_inputs(seed, part) draws one part's arguments, and reference() takes and returns one part's arrays. A program takes and returns all parts, laid end to end along the dimension named above; an argument that names none is the same for every part. Nothing has to cross between parts.
All inputs are finite; a program needn't handle non-finite values.
Results may differ from the reference program's by a relative error of at most 0.017.
Values may be sent and summed in bfloat16 or wider, within the bound.
A program may use at most 64 MiB of HBM per device.

```python
import jax
import jax.numpy as jnp
from jax import lax

DH = 512
HEADS = 2
NS_STEPS = 2
GROUP = 2048


def draw_rates(key, part):
    ramp = 1.0 + 2.0 * jnp.arange(GROUP, dtype=jnp.float32) / (GROUP - 1)
    base = jnp.exp(jax.random.uniform(key, (HEADS, GROUP), jnp.float32, jnp.log(0.3), 0.0))
    return jnp.clip(base * ramp[None, :], 0.3, 3.0)


def levels(own_key, shape, shards, low, largest):
    factor_of = 1.0
    for axis_at, blocks in shards:
        draws = jax.random.uniform(jax.random.fold_in(jax.random.fold_in(own_key, 6), axis_at), (blocks,), jnp.float32, low / len(shards), largest / len(shards))
        factor_of = factor_of * jnp.repeat(jnp.exp(draws), shape[axis_at] // blocks).reshape((-1,) + (1,) * (len(shape) - 1 - axis_at))
    return factor_of


def scatter_about(stream_key, shape, scale, reach, cuts=(), held_as=jnp.bfloat16):
    values = jax.random.normal(stream_key, shape, jnp.float32) * scale
    if len(cuts) > 0:
        values = levels(stream_key, shape, cuts, -0.22, 0.18) * values
    return jnp.clip(values, min=-reach, max=reach).astype(held_as)


def setup_inputs(seed: int = 0, part: int = 0) -> dict:
    arg_keys = jax.random.split(jax.random.key(seed), 6)
    own_keys = jax.random.split(jax.random.fold_in(arg_keys[5], part), 6)
    return {
        "keys": scatter_about(own_keys[0], (GROUP, HEADS * DH), 1.0, 6.0, ((0, 16),)),
        "values": scatter_about(own_keys[1], (GROUP, HEADS * DH), 1.0, 6.0, ((0, 16),)),
        "queries": scatter_about(own_keys[2], (GROUP, HEADS * DH), 1.0, 6.0, ((0, 16),)),
        "rates": draw_rates(jax.random.fold_in(jax.random.fold_in(arg_keys[5], part), 71), part),
        "fast_weights": scatter_about(arg_keys[4], (HEADS, 3, DH, DH), DH ** -0.5, 0.25),
    }


def swiglu_grads(key_rows, value_rows, rate_col, gate_w, up_w, down_w):
    gate = jnp.dot(key_rows, gate_w, preferred_element_type=jnp.float32)
    upper = jnp.dot(key_rows, up_w, preferred_element_type=jnp.float32)
    sigma = jax.nn.sigmoid(gate)
    silu_gate = gate * sigma
    hidden = (silu_gate * upper).astype(jnp.bfloat16)
    outer = (-rate_col[:, None] * value_rows.astype(jnp.float32)).astype(jnp.bfloat16)
    back = jnp.dot(outer, down_w.T, preferred_element_type=jnp.float32)
    d_gate = (back * upper * sigma * (1.0 + gate * (1.0 - sigma))).astype(jnp.bfloat16)
    d_upper = (back * silu_gate).astype(jnp.bfloat16)
    grad_gate = jnp.dot(key_rows.T, d_gate, preferred_element_type=jnp.float32)
    grad_upper = jnp.dot(key_rows.T, d_upper, preferred_element_type=jnp.float32)
    grad_down = jnp.dot(hidden.T, outer, preferred_element_type=jnp.float32)
    return jnp.stack([grad_gate, grad_upper, grad_down])

def newton_schulz(matrix):
    wide = matrix.astype(jnp.float32)
    iterate = (wide / (jnp.sqrt(jnp.sum(wide * wide)) + 1e-07)).astype(jnp.bfloat16)
    for step in range(NS_STEPS):
        gram = jnp.dot(iterate, iterate.T, preferred_element_type=jnp.float32).astype(jnp.bfloat16)
        square = jnp.dot(gram, gram, preferred_element_type=jnp.float32)
        mixed = (-4.775 * gram.astype(jnp.float32) + 2.0315 * square).astype(jnp.bfloat16)
        iterate = (3.4445 * iterate.astype(jnp.float32) + jnp.dot(mixed, iterate, preferred_element_type=jnp.float32)).astype(jnp.bfloat16)
    return iterate

def renormed(weight, update):
    old = weight.astype(jnp.float32)
    fresh = old - update.astype(jnp.float32)
    scale = jnp.sqrt((lax.optimization_barrier(jnp.mean(old * old, axis=1, keepdims=True)) + 1e-06) / (lax.optimization_barrier(jnp.mean(fresh * fresh, axis=1, keepdims=True)) + 1e-06))
    return (fresh * scale).astype(jnp.bfloat16)

def apply_fast(query_rows, gate_w, up_w, down_w):
    gate = jnp.dot(query_rows, gate_w, preferred_element_type=jnp.float32)
    upper = jnp.dot(query_rows, up_w, preferred_element_type=jnp.float32)
    hidden = (jax.nn.silu(gate) * upper).astype(jnp.bfloat16)
    return jnp.dot(hidden, down_w, preferred_element_type=jnp.float32).astype(jnp.bfloat16)

def reference(keys, values, queries, rates, fast_weights):
    outputs = []
    weights_out = []
    for head in range(HEADS):
        cols = slice(head * DH, (head + 1) * DH)
        gate_w = fast_weights[head, 0]
        up_w = fast_weights[head, 1]
        down_w = fast_weights[head, 2]
        grads = swiglu_grads(keys[:, cols], values[:, cols], rates[head], gate_w, up_w, down_w)
        rounded = grads.astype(jnp.bfloat16)
        fresh = [renormed(fast_weights[head, which], newton_schulz(rounded[which])) for which in range(3)]
        weights_out.append(jnp.stack(fresh))
        outputs.append(apply_fast(queries[:, cols], fresh[0], fresh[1], fresh[2]))
    return (jnp.concatenate(outputs, axis=1), jnp.stack(weights_out))
```

```python
import functools

import jax
import jax.numpy as jnp
from jax import lax
from jax.experimental import pallas as pl
from jax.experimental.pallas import tpu as pltpu
from jax.sharding import PartitionSpec as P

HEADS = 2
NS_STEPS = 2
CHUNKS = 4
MESH = pl.DeviceIdType.MESH
F32 = jnp.float32
BF16 = jnp.bfloat16


def dot(a, b):
    return jnp.dot(a, b, preferred_element_type=F32)


def dot_nt(a, b):
    return lax.dot_general(a, b, (((1,), (1,)), ((), ())), preferred_element_type=F32)


def dot_tn(a, b):
    return lax.dot_general(a, b, (((0,), (0,)), ((), ())), preferred_element_type=F32)


def kernel(
    Z, Y,
    k_ref, v_ref, q_ref, r_ref, w_ref,
    out_ref, neww_ref,
    o_loc, left, right, recv, sendbuf, m_buf, ss_buf, x_buf, g_buf, wn,
    tok_send, tok_recv, chain_send, chain_recv, w_send, w_recv, out_sem,
):
    tokens = k_ref.shape[0]
    D = w_ref.shape[2]
    R = D // CHUNKS
    PEERS = 2 * Y
    me = lax.axis_index("tok")
    c = me % 2
    y = (me // 2) % Y
    z = me // PEERS
    mine = y * 2 + c
    mid = Z // 2 - 1

    def at(zz, yy, cc):
        return {"tok": (zz * Y + yy) * 2 + cc}

    barrier = pltpu.get_barrier_semaphore()
    for d in range(1, PEERS):
        peer = z * PEERS + (mine + d) % PEERS
        pl.semaphore_signal(barrier, inc=1, device_id={"tok": peer}, device_id_type=MESH)

    @pl.when(z > 0)
    def _():
        pl.semaphore_signal(barrier, inc=1, device_id={"tok": me - PEERS}, device_id_type=MESH)

    @pl.when(z < Z - 1)
    def _():
        pl.semaphore_signal(barrier, inc=1, device_id={"tok": me + PEERS}, device_id_type=MESH)

    for h in range(HEADS):
        row = jnp.broadcast_to(r_ref[h : h + 1, :], (128, tokens))
        col = jnp.concatenate([row.T] * (D // 128), axis=1)
        o_loc[h] = (-col * v_ref[:, h * D : (h + 1) * D].astype(F32)).astype(BF16)

    own_rows = pl.ds(pl.multiple_of(mine * tokens, tokens), tokens)
    own_cols = pl.ds(pl.multiple_of(c * D, D), D)
    left[0, own_rows, :] = k_ref[:, own_cols]
    right[2, own_rows, :] = o_loc[c]

    pl.semaphore_wait(
        barrier, (PEERS - 1) + jnp.where(z > 0, 1, 0) + jnp.where(z < Z - 1, 1, 0)
    )

    def token_copies(d):
        p = (mine + d) % PEERS
        cc = p % 2
        dev = {"tok": z * PEERS + p}
        cols = pl.ds(pl.multiple_of(cc * D, D), D)
        return (
            pltpu.make_async_remote_copy(
                k_ref.at[:, cols], left.at[0, own_rows, :],
                tok_send.at[0, d - 1], tok_recv.at[0, d - 1],
                device_id=dev, device_id_type=MESH),
            pltpu.make_async_remote_copy(
                o_loc.at[cc], right.at[2, own_rows, :],
                tok_send.at[1, d - 1], tok_recv.at[1, d - 1],
                device_id=dev, device_id_type=MESH),
        )

    for d in range(1, PEERS):
        for cp in token_copies(d):
            cp.start()

    def forward_block(d, _):
        @pl.when(d > 0)
        def _():
            for cp in token_copies(d):
                cp.wait_recv()

        p = (mine + PEERS - d) % PEERS
        rows = pl.ds(pl.multiple_of(p * tokens, tokens), tokens)
        key = left[0, rows, :]
        gate = dot(key, w_ref[c, 0])
        upper = dot(key, w_ref[c, 1])
        back = dot_nt(right[2, rows, :], w_ref[c, 2])
        sigma = jax.nn.sigmoid(gate)
        silu_gate = gate * sigma
        left[1, rows, :] = (silu_gate * upper).astype(BF16)
        right[0, rows, :] = (back * upper * sigma * (1.0 + gate * (1.0 - sigma))).astype(BF16)
        right[1, rows, :] = (back * silu_gate).astype(BF16)
        return 0

    lax.fori_loop(0, PEERS, forward_block, 0)

    same = y == c
    w0 = jnp.where(y == 0, 0, jnp.where(c == 0, 2, 1))
    w1 = jnp.where(y == 0, 1, 2)
    own0 = jnp.where(same, 0, mid)
    own1 = Z - 1
    active0 = y < 2
    active1 = jnp.logical_and(same, y < 2)
    is_owner0 = jnp.logical_and(active0, z == own0)
    is_owner1 = jnp.logical_and(active1, z == own1)
    is_owner = jnp.logical_or(is_owner0, is_owner1)
    owned_w = jnp.where(is_owner1, w1, w0)

    def chain_copy(slot, i, step, side):
        return pltpu.make_async_remote_copy(
            sendbuf.at[slot, i], recv.at[side, slot, i],
            chain_send.at[slot, i], chain_recv.at[side, slot, i],
            device_id={"tok": me + step * PEERS}, device_id_type=MESH)

    def take(side, slot, i):
        chain_copy(slot, i, 1, side).wait_recv()
        part[...] += recv[side, slot, i].astype(F32)

    part = x_buf.at[0, pl.ds(0, R), :]

    def reduce_event(slot, i):
        w = jnp.where(slot == 0, w0, w1)
        own = jnp.where(slot == 0, own0, own1)
        cols = pl.ds(pl.multiple_of(i * R, R), R)
        part[...] = dot_tn(left[jnp.where(w == 2, 1, 0), :, cols], right[w])

        @pl.when(jnp.logical_and(z > 0, z <= own))
        def _():
            take(0, slot, i)

        @pl.when(jnp.logical_and(z < Z - 1, z >= own))
        def _():
            take(1, slot, i)

        @pl.when(z == own)
        def _():
            rounded = part[...].astype(BF16)
            m_buf[cols, :] = rounded
            wide = rounded.astype(F32)
            ss_buf[cols, :] = jnp.sum(wide * wide, axis=1, keepdims=True)

        @pl.when(z != own)
        def _():
            sendbuf[slot, i] = part[...].astype(BF16)

        @pl.when(z < own)
        def _():
            chain_copy(slot, i, 1, 0).start()

        @pl.when(z > own)
        def _():
            chain_copy(slot, i, -1, 1).start()

    near = jnp.where(z < Z // 2, 1, 0)
    first = jnp.where(active1, near, 0)
    lag = jnp.where(jnp.logical_or(z == 0, z == Z - 1), CHUNKS, 1)

    def reduce_step(t, _):
        @pl.when(t < CHUNKS)
        def _():
            reduce_event(first, t)

        @pl.when(jnp.logical_and(active1, jnp.logical_and(t >= lag, t < lag + CHUNKS)))
        def _():
            reduce_event(1 - first, t - lag)

        return 0

    @pl.when(active0)
    def _():
        lax.fori_loop(0, 2 * CHUNKS, reduce_step, 0)

    def place(w, h):
        col = jnp.where(w + h >= 2, 1, 0)
        own = jnp.where(
            col == h,
            jnp.where(w == h, 0, Z - 1),
            mid,
        )
        return col, own

    def w_copies(w, i, go):
        col, own = place(w, c)
        rows = pl.ds(pl.multiple_of(i * R, R), R)
        block = wn.at[c, w, rows, :]
        in_col = y == col

        def copy(kind, dev):
            cp = pltpu.make_async_remote_copy(
                block, block, w_send.at[w, i, kind], w_recv.at[c, w, i],
                device_id=dev, device_id_type=MESH)
            cp.start() if go else cp.wait_send()

        @pl.when(jnp.logical_and(in_col, jnp.logical_and(z >= own, z < Z - 1)))
        def _():
            copy(0, {"tok": me + PEERS})

        @pl.when(jnp.logical_and(in_col, jnp.logical_and(z <= own, z > 0)))
        def _():
            copy(1, {"tok": me - PEERS})

        @pl.when(in_col)
        def _():
            for dy in range(1, Y):
                copy(2 + dy, at(z, (y + dy) % Y, c))

        copy(2, at(z, y, 1 - c))

    def wait_block(h, w, i):
        rows = pl.ds(pl.multiple_of(i * R, R), R)
        block = wn.at[h, w, rows, :]
        pltpu.make_async_remote_copy(
            block, block, w_send.at[w, i, 2], w_recv.at[h, w, i],
            device_id=at(z, y, 1 - c), device_id_type=MESH).wait_recv()

    @pl.when(is_owner)
    def _():
        norm = jnp.sqrt(jnp.sum(ss_buf[...])) + 1e-07
        m_buf[...] = (m_buf[...].astype(F32) / norm).astype(BF16)
        for step in range(NS_STEPS):
            x = m_buf[...]
            g_buf[...] = dot_nt(x, x).astype(BF16)
            g = g_buf[...]
            mixed = (-4.775 * g.astype(F32) + 2.0315 * dot(g, g)).astype(BF16)
            x_buf[0] = 3.4445 * x.astype(F32) + dot(mixed, x)
            m_buf[...] = x_buf[0].astype(BF16)
        for i in range(CHUNKS):
            rows = slice(i * R, (i + 1) * R)
            old = w_ref[c, owned_w, rows, :].astype(F32)
            fresh = old - m_buf[rows, :].astype(F32)
            scale = jnp.sqrt(
                (jnp.mean(old * old, axis=1, keepdims=True) + 1e-06)
                / (jnp.mean(fresh * fresh, axis=1, keepdims=True) + 1e-06)
            )
            wn[c, owned_w, rows, :] = (fresh * scale).astype(BF16)
            w_copies(owned_w, i, True)

    def event(w, i, here):
        col, own = place(w, c)
        owner = jnp.logical_and(y == col, z == own)

        @pl.when(jnp.logical_and((y == col) == here, jnp.logical_not(owner)))
        def _():
            wait_block(c, w, i)
            w_copies(w, i, True)

    def spread(t, _):
        @pl.when(t < CHUNKS)
        def _():
            for w in range(3):
                event(jnp.where(z < Z // 2, w, 2 - w), t, True)

        @pl.when(t > 0)
        def _():
            for w in range(3):
                event(w, t - 1, False)

        return 0

    lax.fori_loop(0, CHUNKS + 1, spread, 0)

    def apply(h):
        cols = pl.ds(pl.multiple_of(h * D, D), D)
        query = q_ref[:, cols]
        gate = dot(query, wn[h, 0])
        upper = dot(query, wn[h, 1])
        hidden = (gate * jax.nn.sigmoid(gate) * upper).astype(BF16)
        out_ref[:, cols] = dot(hidden, wn[h, 2]).astype(BF16)

    def save(h, at_sem):
        return pltpu.make_async_copy(wn.at[h], neww_ref.at[h], out_sem.at[at_sem])

    save(c, 0).start()

    def turn(s, _):
        @pl.when(s == 1)
        def _():
            def wait_all(i, _):
                for w in range(3):
                    wait_block(1 - c, w, i)
                return 0

            lax.fori_loop(0, CHUNKS, wait_all, 0)
            save(1 - c, 1).start()

        apply(jnp.where(s == 0, c, 1 - c))
        return 0

    lax.fori_loop(0, 2, turn, 0)

    for d in range(1, PEERS):
        for cp in token_copies(d):
            cp.wait_send()

    def drain(i, _):
        @pl.when(jnp.logical_and(active0, z != own0))
        def _():
            chain_copy(0, i, 1, 0).wait_send()

        @pl.when(jnp.logical_and(active1, z != own1))
        def _():
            chain_copy(1, i, 1, 0).wait_send()

        for w in range(3):
            w_copies(w, i, False)
        return 0

    lax.fori_loop(0, CHUNKS, drain, 0)
    save(c, 0).wait()
    save(1 - c, 1).wait()


def body(Z, Y, keys, values, queries, rates, fast_weights):
    D = fast_weights.shape[2]
    tokens = keys.shape[0]
    rows = tokens * 2 * Y
    vmem = pl.BlockSpec(memory_space=pltpu.VMEM)

    def run(*refs):
        kernel(Z, Y, *refs)

    return pl.pallas_call(
        run,
        out_shape=(
            jax.ShapeDtypeStruct((tokens, HEADS * D), BF16),
            jax.ShapeDtypeStruct((HEADS, 3, D, D), BF16),
        ),
        in_specs=[vmem] * 5,
        out_specs=(vmem, pl.BlockSpec(memory_space=pl.ANY)),
        scratch_shapes=[
            pltpu.VMEM((HEADS, tokens, D), BF16),
            pltpu.VMEM((2, rows, D), BF16),
            pltpu.VMEM((3, rows, D), BF16),
            pltpu.VMEM((2, 2, CHUNKS, D // CHUNKS, D), BF16),
            pltpu.VMEM((2, CHUNKS, D // CHUNKS, D), BF16),
            pltpu.VMEM((D, D), BF16),
            pltpu.VMEM((D, 1), F32),
            pltpu.VMEM((1, D, D), F32),
            pltpu.VMEM((D, D), BF16),
            pltpu.VMEM((HEADS, 3, D, D), BF16),
            pltpu.SemaphoreType.DMA((2, 2 * Y - 1)),
            pltpu.SemaphoreType.DMA((2, 2 * Y - 1)),
            pltpu.SemaphoreType.DMA((2, CHUNKS)),
            pltpu.SemaphoreType.DMA((2, 2, CHUNKS)),
            pltpu.SemaphoreType.DMA((3, CHUNKS, 2 + Y)),
            pltpu.SemaphoreType.DMA((HEADS, 3, CHUNKS)),
            pltpu.SemaphoreType.DMA((2,)),
        ],
        compiler_params=pltpu.CompilerParams(
            collective_id=0, has_side_effects=True, vmem_limit_bytes=56 * 1024 * 1024
        ),
        name="ttt_step",
    )(keys, values, queries, rates, fast_weights)


def solution(mesh):
    chips = mesh.shape["tok"] // 2
    Y = 1
    while Y * Y * 4 <= chips and chips % (2 * Y) == 0:
        Y *= 2
    Z = chips // Y
    return jax.shard_map(
        functools.partial(body, Z, Y),
        mesh=mesh,
        in_specs=(
            P(("grp", "tok"), None),
            P(("grp", "tok"), None),
            P(("grp", "tok"), None),
            P(None, ("grp", "tok")),
            P(),
        ),
        out_specs=(P(("grp", "tok"), None), P("grp", None, None, None)),
        check_vma=False,
    )
```

```python
import functools

import jax
import jax.numpy as jnp
from jax import lax
from jax.experimental import pallas as pl
from jax.experimental.pallas import tpu as pltpu
from jax.sharding import PartitionSpec as P

HEADS = 2
NS_STEPS = 2
CHUNKS = 8
SUM_CHUNKS = 4
SUM_LAG = 2
LAG = 3
BOTH = 4
MESH = pl.DeviceIdType.MESH
F32 = jnp.float32
BF16 = jnp.bfloat16


def dot(a, b):
    return jnp.dot(a, b, preferred_element_type=F32)


def dot_nt(a, b):
    return lax.dot_general(a, b, (((1,), (1,)), ((), ())), preferred_element_type=F32)


def dot_tn(a, b):
    return lax.dot_general(a, b, (((0,), (0,)), ((), ())), preferred_element_type=F32)


def kernel(
    Z, Y,
    k_hbm, v_hbm, q_hbm, r_hbm, w_hbm,
    out_ref, neww_ref,
    v_ref, q_ref, r_ref, w_ref,
    o_loc, left, right, recv, sendbuf, m_buf, ss_buf, x_buf, g_buf, wn,
    tok_send, tok_recv, chain_send, chain_recv, w_send, w_recv, out_sem, in_sem,
):
    tokens = k_hbm.shape[0]
    D = w_ref.shape[2]
    R = D // CHUNKS
    RS = D // SUM_CHUNKS
    PEERS = 2 * Y
    me = lax.axis_index("tok")
    c = me % 2
    y = (me // 2) % Y
    z = me // PEERS
    mine = y * 2 + c
    mid = Z // 2 - 1

    def at(zz, yy, cc):
        return {"tok": (zz * Y + yy) * 2 + cc}

    own_rows = pl.ds(pl.multiple_of(mine * tokens, tokens), tokens)
    own_cols = pl.ds(pl.multiple_of(c * D, D), D)
    loads = [
        pltpu.make_async_copy(src, dst, in_sem.at[n])
        for n, (src, dst) in enumerate((
            (r_hbm, r_ref), (v_hbm, v_ref), (k_hbm.at[:, own_cols], left.at[0, own_rows, :]),
            (w_hbm.at[c], w_ref.at[c]), (q_hbm, q_ref),
        ))
    ]
    for load in loads:
        load.start()

    barrier = pltpu.get_barrier_semaphore()
    for d in range(1, PEERS):
        peer = z * PEERS + (mine + d) % PEERS
        pl.semaphore_signal(barrier, inc=1, device_id={"tok": peer}, device_id_type=MESH)

    @pl.when(z > 0)
    def _():
        pl.semaphore_signal(barrier, inc=1, device_id={"tok": me - PEERS}, device_id_type=MESH)

    @pl.when(z < Z - 1)
    def _():
        pl.semaphore_signal(barrier, inc=1, device_id={"tok": me + PEERS}, device_id_type=MESH)

    loads[0].wait()
    loads[1].wait()
    for h in range(HEADS):
        row = jnp.broadcast_to(r_ref[h : h + 1, :], (128, tokens))
        col = jnp.concatenate([row.T] * (D // 128), axis=1)
        o_loc[h] = (-col * v_ref[:, h * D : (h + 1) * D].astype(F32)).astype(BF16)

    right[2, own_rows, :] = o_loc[c]

    pl.semaphore_wait(
        barrier, (PEERS - 1) + jnp.where(z > 0, 1, 0) + jnp.where(z < Z - 1, 1, 0)
    )

    def token_copies(d):
        p = (mine + d) % PEERS
        cc = p % 2
        dev = {"tok": z * PEERS + p}
        cols = pl.ds(pl.multiple_of(cc * D, D), D)
        return (
            pltpu.make_async_remote_copy(
                k_hbm.at[:, cols], left.at[0, own_rows, :],
                tok_send.at[0, d - 1], tok_recv.at[0, d - 1],
                device_id=dev, device_id_type=MESH),
            pltpu.make_async_remote_copy(
                o_loc.at[cc], right.at[2, own_rows, :],
                tok_send.at[1, d - 1], tok_recv.at[1, d - 1],
                device_id=dev, device_id_type=MESH),
        )

    for d in range(1, PEERS):
        for cp in token_copies(d):
            cp.start()

    loads[2].wait()
    loads[3].wait()

    def forward_block(d, _):
        @pl.when(d > 0)
        def _():
            for cp in token_copies(d):
                cp.wait_recv()

        p = (mine + PEERS - d) % PEERS
        rows = pl.ds(pl.multiple_of(p * tokens, tokens), tokens)
        key = left[0, rows, :]
        gate = dot(key, w_ref[c, 0])
        upper = dot(key, w_ref[c, 1])
        back = dot_nt(right[2, rows, :], w_ref[c, 2])
        sigma = jax.nn.sigmoid(gate)
        silu_gate = gate * sigma
        left[1, rows, :] = (silu_gate * upper).astype(BF16)
        right[0, rows, :] = (back * upper * sigma * (1.0 + gate * (1.0 - sigma))).astype(BF16)
        right[1, rows, :] = (back * silu_gate).astype(BF16)
        return 0

    lax.fori_loop(0, PEERS, forward_block, 0)

    same = y == c
    w0 = jnp.where(y == 0, 0, jnp.where(c == 0, 2, 1))
    w1 = jnp.where(y == 0, 1, 2)
    own0 = jnp.where(same, 0, mid)
    own1 = Z - 1
    active0 = y < 2
    active1 = jnp.logical_and(same, y < 2)
    is_owner0 = jnp.logical_and(active0, z == own0)
    is_owner1 = jnp.logical_and(active1, z == own1)
    is_owner = jnp.logical_or(is_owner0, is_owner1)
    owned_w = jnp.where(is_owner1, w1, w0)

    def chain_copy(slot, i, step, side):
        return pltpu.make_async_remote_copy(
            sendbuf.at[slot, i], recv.at[side, slot, i],
            chain_send.at[slot, i], chain_recv.at[side, slot, i],
            device_id={"tok": me + step * PEERS}, device_id_type=MESH)

    def take(side, slot, i):
        chain_copy(slot, i, 1, side).wait_recv()
        part[...] += recv[side, slot, i].astype(F32)

    part = x_buf.at[0, pl.ds(0, RS), :]

    def reduce_event(slot, i):
        w = jnp.where(slot == 0, w0, w1)
        own = jnp.where(slot == 0, own0, own1)
        cols = pl.ds(pl.multiple_of(i * RS, RS), RS)
        part[...] = dot_tn(left[jnp.where(w == 2, 1, 0), :, cols], right[w])

        @pl.when(jnp.logical_and(z > 0, z <= own))
        def _():
            take(0, slot, i)

        @pl.when(jnp.logical_and(z < Z - 1, z >= own))
        def _():
            take(1, slot, i)

        @pl.when(z == own)
        def _():
            rounded = part[...].astype(BF16)
            m_buf[cols, :] = rounded
            wide = rounded.astype(F32)
            ss_buf[cols, :] = jnp.sum(wide * wide, axis=1, keepdims=True)

        @pl.when(z != own)
        def _():
            sendbuf[slot, i] = part[...].astype(BF16)

        @pl.when(z < own)
        def _():
            chain_copy(slot, i, 1, 0).start()

        @pl.when(z > own)
        def _():
            chain_copy(slot, i, -1, 1).start()

    def depth(own):
        rise = jnp.where(z <= own, z, 0)
        fall = jnp.where(z >= own, Z - 1 - z, 0)
        return SUM_LAG * jnp.maximum(rise, fall)

    near = jnp.where(z < Z // 2, 1, 0)
    first = jnp.where(active1, near, 0)
    lag_first = depth(jnp.where(first == 0, own0, own1))
    lag_last = depth(jnp.where(first == 0, own1, own0))

    def reduce_step(t, _):
        @pl.when(jnp.logical_and(t >= lag_first, t < lag_first + SUM_CHUNKS))
        def _():
            reduce_event(first, t - lag_first)

        @pl.when(jnp.logical_and(active1, jnp.logical_and(t >= lag_last, t < lag_last + SUM_CHUNKS)))
        def _():
            reduce_event(1 - first, t - lag_last)

        return 0

    @pl.when(active0)
    def _():
        lax.fori_loop(0, SUM_CHUNKS + SUM_LAG * (Z - 1), reduce_step, 0)

    def place(w, h):
        col = jnp.where(w + h >= 2, 1, 0)
        own = jnp.where(
            col == h,
            jnp.where(w == h, 0, Z - 1),
            mid,
        )
        return col, own

    def w_copies(w, i, go):
        col, own = place(w, c)
        rows = pl.ds(pl.multiple_of(i * R, R), R)
        block = wn.at[c, w, rows, :]
        in_col = y == col
        both = i % BOTH == BOTH - 1
        along = jnp.logical_or(in_col, both)

        def copy(kind, dev):
            cp = pltpu.make_async_remote_copy(
                block, block, w_send.at[w, i, kind], w_recv.at[c, w, i],
                device_id=dev, device_id_type=MESH)
            cp.start() if go else cp.wait_send()

        @pl.when(jnp.logical_and(along, jnp.logical_and(z >= own, z < Z - 1)))
        def _():
            copy(0, {"tok": me + PEERS})

        @pl.when(jnp.logical_and(along, jnp.logical_and(z <= own, z > 0)))
        def _():
            copy(1, {"tok": me - PEERS})

        @pl.when(jnp.logical_and(in_col, jnp.logical_or(jnp.logical_not(both), z == own)))
        def _():
            for dy in range(1, Y):
                copy(2 + dy, at(z, (y + dy) % Y, c))

        copy(2, at(z, y, 1 - c))

    def wait_block(h, w, i):
        rows = pl.ds(pl.multiple_of(i * R, R), R)
        block = wn.at[h, w, rows, :]
        pltpu.make_async_remote_copy(
            block, block, w_send.at[w, i, 2], w_recv.at[h, w, i],
            device_id=at(z, y, 1 - c), device_id_type=MESH).wait_recv()

    @pl.when(is_owner)
    def _():
        norm = jnp.sqrt(jnp.sum(ss_buf[...])) + 1e-07
        m_buf[...] = (m_buf[...].astype(F32) / norm).astype(BF16)
        for step in range(NS_STEPS):
            x = m_buf[...]
            g_buf[...] = dot_nt(x, x).astype(BF16)
            g = g_buf[...]
            mixed = (-4.775 * g.astype(F32) + 2.0315 * dot(g, g)).astype(BF16)
            x_buf[0] = 3.4445 * x.astype(F32) + dot(mixed, x)
            m_buf[...] = x_buf[0].astype(BF16)
        for i in range(CHUNKS):
            rows = slice(i * R, (i + 1) * R)
            old = w_ref[c, owned_w, rows, :].astype(F32)
            fresh = old - m_buf[rows, :].astype(F32)
            scale = jnp.sqrt(
                (jnp.mean(old * old, axis=1, keepdims=True) + 1e-06)
                / (jnp.mean(fresh * fresh, axis=1, keepdims=True) + 1e-06)
            )
            wn[c, owned_w, rows, :] = (fresh * scale).astype(BF16)
            w_copies(owned_w, i, True)

    def spread(t, _):
        for n in range(3):
            w = jnp.where(z < Z // 2, n, 2 - n)
            col, own = place(w, c)
            hops = jnp.abs(z - own) + jnp.where(y == col, 0, 1)
            i = t - LAG * (hops - 1)

            @pl.when(jnp.logical_and(hops > 0, jnp.logical_and(i >= 0, i < CHUNKS)))
            def _():
                wait_block(c, w, i)
                w_copies(w, i, True)

        return 0

    lax.fori_loop(0, CHUNKS + LAG * (Z - 1), spread, 0)

    def apply(h):
        cols = pl.ds(pl.multiple_of(h * D, D), D)
        query = q_ref[:, cols]
        gate = dot(query, wn[h, 0])
        upper = dot(query, wn[h, 1])
        hidden = (gate * jax.nn.sigmoid(gate) * upper).astype(BF16)
        out_ref[:, cols] = dot(hidden, wn[h, 2]).astype(BF16)

    def save(h, at_sem):
        return pltpu.make_async_copy(wn.at[h], neww_ref.at[h], out_sem.at[at_sem])

    save(c, 0).start()

    def turn(s, _):
        @pl.when(s == 1)
        def _():
            def wait_all(i, _):
                for w in range(3):
                    wait_block(1 - c, w, i)
                return 0

            lax.fori_loop(0, CHUNKS, wait_all, 0)
            save(1 - c, 1).start()

        apply(jnp.where(s == 0, c, 1 - c))
        return 0

    loads[4].wait()
    lax.fori_loop(0, 2, turn, 0)

    for d in range(1, PEERS):
        for cp in token_copies(d):
            cp.wait_send()

    def drain_sums(i, _):
        @pl.when(jnp.logical_and(active0, z != own0))
        def _():
            chain_copy(0, i, 1, 0).wait_send()

        @pl.when(jnp.logical_and(active1, z != own1))
        def _():
            chain_copy(1, i, 1, 0).wait_send()

        return 0

    lax.fori_loop(0, SUM_CHUNKS, drain_sums, 0)

    def drain(i, _):
        for w in range(3):
            w_copies(w, i, False)
        return 0

    lax.fori_loop(0, CHUNKS, drain, 0)
    save(c, 0).wait()
    save(1 - c, 1).wait()


def store(a_ref, b_ref, a_out, b_out, sem):
    copies = [
        pltpu.make_async_copy(b_ref, b_out, sem.at[0]),
        pltpu.make_async_copy(a_ref, a_out, sem.at[1]),
    ]
    for cp in copies:
        cp.start()
    for cp in copies:
        cp.wait()


def body(Z, Y, keys, values, queries, rates, fast_weights):
    D = fast_weights.shape[2]
    tokens = keys.shape[0]
    rows = tokens * 2 * Y
    vmem = pl.BlockSpec(memory_space=pltpu.VMEM)
    hbm = pl.BlockSpec(memory_space=pltpu.MemorySpace.HBM)

    def run(*refs):
        kernel(Z, Y, *refs)

    out, fresh = pl.pallas_call(
        run,
        out_shape=(
            jax.ShapeDtypeStruct((tokens, HEADS * D), BF16),
            jax.ShapeDtypeStruct((HEADS, 3, D, D), BF16),
        ),
        in_specs=[hbm] * 5,
        out_specs=(vmem, pl.BlockSpec(memory_space=pl.ANY)),
        scratch_shapes=[
            pltpu.VMEM((tokens, HEADS * D), BF16),
            pltpu.VMEM((tokens, HEADS * D), BF16),
            pltpu.VMEM(rates.shape, F32),
            pltpu.VMEM((HEADS, 3, D, D), BF16),
            pltpu.VMEM((HEADS, tokens, D), BF16),
            pltpu.VMEM((2, rows, D), BF16),
            pltpu.VMEM((3, rows, D), BF16),
            pltpu.VMEM((2, 2, SUM_CHUNKS, D // SUM_CHUNKS, D), BF16),
            pltpu.VMEM((2, SUM_CHUNKS, D // SUM_CHUNKS, D), BF16),
            pltpu.VMEM((D, D), BF16),
            pltpu.VMEM((D, 1), F32),
            pltpu.VMEM((1, D, D), F32),
            pltpu.VMEM((D, D), BF16),
            pltpu.VMEM((HEADS, 3, D, D), BF16),
            pltpu.SemaphoreType.DMA((2, 2 * Y - 1)),
            pltpu.SemaphoreType.DMA((2, 2 * Y - 1)),
            pltpu.SemaphoreType.DMA((2, SUM_CHUNKS)),
            pltpu.SemaphoreType.DMA((2, 2, SUM_CHUNKS)),
            pltpu.SemaphoreType.DMA((3, CHUNKS, 2 + Y)),
            pltpu.SemaphoreType.DMA((HEADS, 3, CHUNKS)),
            pltpu.SemaphoreType.DMA((2,)),
            pltpu.SemaphoreType.DMA((5,)),
        ],
        compiler_params=pltpu.CompilerParams(
            collective_id=0, has_side_effects=True, vmem_limit_bytes=30 * 1024 * 1024
        ),
        name="ttt_step",
    )(*[pltpu.with_memory_space_constraint(a, pltpu.MemorySpace.HBM) for a in (keys, values, queries, rates, fast_weights)])
    anywhere = pl.BlockSpec(memory_space=pl.ANY)
    return pl.pallas_call(
        store,
        out_shape=(
            jax.ShapeDtypeStruct(out.shape, BF16),
            jax.ShapeDtypeStruct(fresh.shape, BF16),
        ),
        in_specs=[anywhere] * 2,
        out_specs=(hbm, hbm),
        scratch_shapes=[pltpu.SemaphoreType.DMA((2,))],
        compiler_params=pltpu.CompilerParams(vmem_limit_bytes=1024 * 1024),
        name="store",
    )(out, fresh)


def solution(mesh):
    chips = mesh.shape["tok"] // 2
    Y = 1
    while Y * Y * 4 <= chips and chips % (2 * Y) == 0:
        Y *= 2
    Z = chips // Y
    return jax.shard_map(
        functools.partial(body, Z, Y),
        mesh=mesh,
        in_specs=(
            P(("grp", "tok"), None),
            P(("grp", "tok"), None),
            P(("grp", "tok"), None),
            P(None, ("grp", "tok")),
            P(),
        ),
        out_specs=(P(("grp", "tok"), None), P("grp", None, None, None)),
        check_vma=False,
    )
```

```python
import functools

import jax
import jax.numpy as jnp
from jax import lax
from jax.experimental import pallas as pl
from jax.experimental.pallas import tpu as pltpu
from jax.sharding import PartitionSpec as P

HEADS = 2
NS_STEPS = 2
CHUNKS = 8
SUM_CHUNKS = 8
HALVES = 2
CROSS = 2
SUM_LAG = 3
LAG = 4
BOTH = 4
SHIFT = 0
MESH = pl.DeviceIdType.MESH
F32 = jnp.float32
BF16 = jnp.bfloat16


def dot(a, b):
    return jnp.dot(a, b, preferred_element_type=F32)


def dot_nt(a, b):
    return lax.dot_general(a, b, (((1,), (1,)), ((), ())), preferred_element_type=F32)


def dot_tn(a, b):
    return lax.dot_general(a, b, (((0,), (0,)), ((), ())), preferred_element_type=F32)


def kernel(
    Z, Y,
    k_hbm, v_hbm, q_hbm, r_hbm, w_hbm,
    out_ref, neww_ref,
    v_ref, q_ref, r_ref, w_ref,
    o_loc, left, right, recv, sendbuf, m_buf, x_buf, g_buf, wn, recv_y,
    tok_send, tok_recv, chain_send, chain_recv, cross_recv, w_send, w_recv, out_sem, in_sem,
):
    tokens = k_hbm.shape[0]
    D = w_ref.shape[2]
    R = D // CHUNKS
    RS = D * HALVES // SUM_CHUNKS
    CS = D // HALVES
    PEERS = 2 * Y
    me = lax.axis_index("tok")
    c = me % 2
    y = (me // 2) % Y
    z = me // PEERS
    mine = y * 2 + c
    mid = Z // 2 - 1

    def at(zz, yy, cc):
        return {"tok": (zz * Y + yy) * 2 + cc}

    own_rows = pl.ds(pl.multiple_of(mine * tokens, tokens), tokens)
    own_cols = pl.ds(pl.multiple_of(c * D, D), D)
    loads = [
        pltpu.make_async_copy(src, dst, in_sem.at[n])
        for n, (src, dst) in enumerate((
            (r_hbm, r_ref), (v_hbm, v_ref), (k_hbm.at[:, own_cols], left.at[0, own_rows, :]),
            (w_hbm.at[c], w_ref.at[c]), (q_hbm, q_ref),
        ))
    ]
    for load in loads:
        load.start()

    barrier = pltpu.get_barrier_semaphore()
    for d in range(1, PEERS):
        peer = z * PEERS + (mine + d) % PEERS
        pl.semaphore_signal(barrier, inc=1, device_id={"tok": peer}, device_id_type=MESH)

    @pl.when(z > 0)
    def _():
        pl.semaphore_signal(barrier, inc=1, device_id={"tok": me - PEERS}, device_id_type=MESH)

    @pl.when(z < Z - 1)
    def _():
        pl.semaphore_signal(barrier, inc=1, device_id={"tok": me + PEERS}, device_id_type=MESH)

    loads[0].wait()
    loads[1].wait()
    for h in range(HEADS):
        row = jnp.broadcast_to(r_ref[h : h + 1, :], (128, tokens))
        col = jnp.concatenate([row.T] * (D // 128), axis=1)
        o_loc[h] = (-col * v_ref[:, h * D : (h + 1) * D].astype(F32)).astype(BF16)

    right[2, own_rows, :] = o_loc[c]

    pl.semaphore_wait(
        barrier, (PEERS - 1) + jnp.where(z > 0, 1, 0) + jnp.where(z < Z - 1, 1, 0)
    )

    def token_copies(d):
        p = (mine + d) % PEERS
        cc = p % 2
        dev = {"tok": z * PEERS + p}
        cols = pl.ds(pl.multiple_of(cc * D, D), D)
        return (
            pltpu.make_async_remote_copy(
                k_hbm.at[:, cols], left.at[0, own_rows, :],
                tok_send.at[0, d - 1], tok_recv.at[0, d - 1],
                device_id=dev, device_id_type=MESH),
            pltpu.make_async_remote_copy(
                o_loc.at[cc], right.at[2, own_rows, :],
                tok_send.at[1, d - 1], tok_recv.at[1, d - 1],
                device_id=dev, device_id_type=MESH),
        )

    def reached(d):
        p = (mine + d) % PEERS
        return jnp.logical_or(p % 2 != CROSS, p // 2 == y)

    for d in range(1, PEERS):

        @pl.when(reached(d))
        def _():
            for cp in token_copies(d):
                cp.start()

    loads[2].wait()
    loads[3].wait()

    def forward_block(d, _):
        p = (mine + PEERS - d) % PEERS

        @pl.when(jnp.logical_or(c != CROSS, p // 2 == y))
        def _():
            forward_rows(d, p)

        return 0

    def forward_rows(d, p):
        @pl.when(d > 0)
        def _():
            for cp in token_copies(d):
                cp.wait_recv()

        rows = pl.ds(pl.multiple_of(p * tokens, tokens), tokens)
        key = left[0, rows, :]
        gate = dot(key, w_ref[c, 0])
        upper = dot(key, w_ref[c, 1])
        back = dot_nt(right[2, rows, :], w_ref[c, 2])
        sigma = jax.nn.sigmoid(gate)
        silu_gate = gate * sigma
        left[1, rows, :] = (silu_gate * upper).astype(BF16)
        right[0, rows, :] = (back * upper * sigma * (1.0 + gate * (1.0 - sigma))).astype(BF16)
        right[1, rows, :] = (back * silu_gate).astype(BF16)

    lax.fori_loop(0, PEERS, forward_block, 0)

    def place(w, h):
        col = jnp.where(w + h >= 2, 1, 0)
        own = jnp.where(
            col == h,
            jnp.where(w == h, 0, Z - 1),
            mid + SHIFT * col,
        )
        return col, own

    def crosses(w):
        return jnp.logical_and(c == CROSS, y != place(w, c)[0])

    def active(w):
        return jnp.logical_or(c == CROSS, y == place(w, c)[0])

    def owns(w):
        col, own = place(w, c)
        return jnp.logical_and(y == col, z == own)

    is_owner = functools.reduce(jnp.logical_or, [owns(w) for w in range(3)])
    owned_w = jnp.where(owns(0), 0, jnp.where(owns(1), 1, 2))

    def chain_copy(w, i, step, side):
        return pltpu.make_async_remote_copy(
            sendbuf.at[w, i], recv.at[side, w, i],
            chain_send.at[w, i], chain_recv.at[side, w, i],
            device_id={"tok": me + step * PEERS}, device_id_type=MESH)

    def cross_copy(w, i, slot):
        return pltpu.make_async_remote_copy(
            sendbuf.at[w, i], recv_y.at[slot, i],
            chain_send.at[w, i], cross_recv.at[slot, i],
            device_id=at(z, place(w, c)[0], c), device_id_type=MESH)

    def take(side, w, i):
        chain_copy(w, i, 1, side).wait_recv()
        part[...] += recv[side, w, i].astype(F32)

    part = x_buf.at[0, pl.ds(0, RS), pl.ds(0, CS)]
    chip_rows = pl.ds(pl.multiple_of(y * 2 * tokens, 2 * tokens), 2 * tokens)

    def reduce_event(w, i):
        col, own = place(w, c)
        rows = pl.ds(pl.multiple_of((i // HALVES) * RS, RS), RS)
        cols = pl.ds(pl.multiple_of((i % HALVES) * CS, CS), CS)
        side_l = 1 if w == 2 else 0

        @pl.when(c != CROSS)
        def _():
            part[...] = dot_tn(left[side_l, :, rows], right[w, :, cols])

        @pl.when(c == CROSS)
        def _():
            part[...] = dot_tn(left[side_l, chip_rows, rows], right[w, chip_rows, cols])

        @pl.when(jnp.logical_and(z > 0, z <= own))
        def _():
            take(0, w, i)

        @pl.when(jnp.logical_and(z < Z - 1, z >= own))
        def _():
            take(1, w, i)

        @pl.when(owns(w))
        def _():
            @pl.when(c == CROSS)
            def _():
                for slot in range(Y - 1):
                    cross_copy(w, i, slot).wait_recv()
                    part[...] += recv_y[slot, i].astype(F32)

            m_buf[rows, cols] = part[...].astype(BF16)

        @pl.when(jnp.logical_not(owns(w)))
        def _():
            sendbuf[w, i] = part[...].astype(BF16)

        @pl.when(z < own)
        def _():
            chain_copy(w, i, 1, 0).start()

        @pl.when(z > own)
        def _():
            chain_copy(w, i, -1, 1).start()

        @pl.when(jnp.logical_and(z == own, crosses(w)))
        def _():
            cross_copy(w, i, (y + Y - col) % Y - 1).start()

    def depth(w):
        own = place(w, c)[1]
        rise = jnp.where(z <= own, z, 0)
        fall = jnp.where(z >= own, Z - 1 - z, 0)
        met = jnp.where(jnp.logical_and(owns(w), c == CROSS), 1, 0)
        return SUM_LAG * (jnp.maximum(rise, fall) + met)

    def reduce_step(t, _):
        for w in range(3):
            i = t - depth(w)

            @pl.when(jnp.logical_and(active(w), jnp.logical_and(i >= 0, i < SUM_CHUNKS)))
            def _():
                reduce_event(w, i)

        return 0

    lax.fori_loop(0, SUM_CHUNKS + SUM_LAG * Z, reduce_step, 0)

    def w_copies(w, i, go):
        col, own = place(w, c)
        rows = pl.ds(pl.multiple_of(i * R, R), R)
        block = wn.at[c, w, rows, :]
        in_col = y == col
        both = i % BOTH == BOTH - 1
        along = jnp.logical_or(in_col, both)

        def copy(kind, dev):
            cp = pltpu.make_async_remote_copy(
                block, block, w_send.at[w, i, kind], w_recv.at[c, w, i],
                device_id=dev, device_id_type=MESH)
            cp.start() if go else cp.wait_send()

        @pl.when(jnp.logical_and(along, jnp.logical_and(z >= own, z < Z - 1)))
        def _():
            copy(0, {"tok": me + PEERS})

        @pl.when(jnp.logical_and(along, jnp.logical_and(z <= own, z > 0)))
        def _():
            copy(1, {"tok": me - PEERS})

        @pl.when(jnp.logical_and(in_col, jnp.logical_or(jnp.logical_not(both), z == own)))
        def _():
            for dy in range(1, Y):
                copy(2 + dy, at(z, (y + dy) % Y, c))

        copy(2, at(z, y, 1 - c))

    def wait_block(h, w, i):
        rows = pl.ds(pl.multiple_of(i * R, R), R)
        block = wn.at[h, w, rows, :]
        pltpu.make_async_remote_copy(
            block, block, w_send.at[w, i, 2], w_recv.at[h, w, i],
            device_id=at(z, y, 1 - c), device_id_type=MESH).wait_recv()

    @pl.when(is_owner)
    def _():
        wide = m_buf[...].astype(F32)
        norm = jnp.sqrt(jnp.sum(wide * wide)) + 1e-07
        m_buf[...] = (wide / norm).astype(BF16)
        for step in range(NS_STEPS):
            x = m_buf[...]
            g_buf[...] = dot_nt(x, x).astype(BF16)
            g = g_buf[...]
            mixed = (-4.775 * g.astype(F32) + 2.0315 * dot(g, g)).astype(BF16)
            x_buf[0] = 3.4445 * x.astype(F32) + dot(mixed, x)
            m_buf[...] = x_buf[0].astype(BF16)
        for i in range(CHUNKS):
            rows = slice(i * R, (i + 1) * R)
            old = w_ref[c, owned_w, rows, :].astype(F32)
            fresh = old - m_buf[rows, :].astype(F32)
            scale = jnp.sqrt(
                (jnp.mean(old * old, axis=1, keepdims=True) + 1e-06)
                / (jnp.mean(fresh * fresh, axis=1, keepdims=True) + 1e-06)
            )
            wn[c, owned_w, rows, :] = (fresh * scale).astype(BF16)
            w_copies(owned_w, i, True)

    def spread(t, _):
        for n in range(3):
            w = jnp.where(z < Z // 2, n, 2 - n)
            col, own = place(w, c)
            hops = jnp.abs(z - own) + jnp.where(y == col, 0, 1)
            i = t - LAG * (hops - 1)

            @pl.when(jnp.logical_and(hops > 0, jnp.logical_and(i >= 0, i < CHUNKS)))
            def _():
                wait_block(c, w, i)
                w_copies(w, i, True)

        return 0

    lax.fori_loop(0, CHUNKS + LAG * (Z - 1), spread, 0)

    def apply(h):
        cols = pl.ds(pl.multiple_of(h * D, D), D)
        query = q_ref[:, cols]
        gate = dot(query, wn[h, 0])
        upper = dot(query, wn[h, 1])
        hidden = (gate * jax.nn.sigmoid(gate) * upper).astype(BF16)
        out_ref[:, cols] = dot(hidden, wn[h, 2]).astype(BF16)

    def save(h, at_sem):
        return pltpu.make_async_copy(wn.at[h], neww_ref.at[h], out_sem.at[at_sem])

    save(c, 0).start()

    def turn(s, _):
        @pl.when(s == 1)
        def _():
            def wait_all(i, _):
                for w in range(3):
                    wait_block(1 - c, w, i)
                return 0

            lax.fori_loop(0, CHUNKS, wait_all, 0)
            save(1 - c, 1).start()

        apply(jnp.where(s == 0, c, 1 - c))
        return 0

    loads[4].wait()
    lax.fori_loop(0, 2, turn, 0)

    for d in range(1, PEERS):

        @pl.when(reached(d))
        def _():
            for cp in token_copies(d):
                cp.wait_send()

    def drain_sums(i, _):
        for w in range(3):

            @pl.when(jnp.logical_and(active(w), jnp.logical_not(owns(w))))
            def _():
                chain_copy(w, i, 1, 0).wait_send()

        return 0

    lax.fori_loop(0, SUM_CHUNKS, drain_sums, 0)

    def drain(i, _):
        for w in range(3):
            w_copies(w, i, False)
        return 0

    lax.fori_loop(0, CHUNKS, drain, 0)
    save(c, 0).wait()
    save(1 - c, 1).wait()


def store(a_ref, b_ref, a_out, b_out, sem):
    copies = [
        pltpu.make_async_copy(b_ref, b_out, sem.at[0]),
        pltpu.make_async_copy(a_ref, a_out, sem.at[1]),
    ]
    for cp in copies:
        cp.start()
    for cp in copies:
        cp.wait()


def body(Z, Y, keys, values, queries, rates, fast_weights):
    D = fast_weights.shape[2]
    tokens = keys.shape[0]
    rows = tokens * 2 * Y
    vmem = pl.BlockSpec(memory_space=pltpu.VMEM)
    hbm = pl.BlockSpec(memory_space=pltpu.MemorySpace.HBM)

    def run(*refs):
        kernel(Z, Y, *refs)

    out, fresh = pl.pallas_call(
        run,
        out_shape=(
            jax.ShapeDtypeStruct((tokens, HEADS * D), BF16),
            jax.ShapeDtypeStruct((HEADS, 3, D, D), BF16),
        ),
        in_specs=[hbm] * 5,
        out_specs=(vmem, pl.BlockSpec(memory_space=pl.ANY)),
        scratch_shapes=[
            pltpu.VMEM((tokens, HEADS * D), BF16),
            pltpu.VMEM((tokens, HEADS * D), BF16),
            pltpu.VMEM(rates.shape, F32),
            pltpu.VMEM((HEADS, 3, D, D), BF16),
            pltpu.VMEM((HEADS, tokens, D), BF16),
            pltpu.VMEM((2, rows, D), BF16),
            pltpu.VMEM((3, rows, D), BF16),
            pltpu.VMEM((2, 3, SUM_CHUNKS, D * HALVES // SUM_CHUNKS, D // HALVES), BF16),
            pltpu.VMEM((3, SUM_CHUNKS, D * HALVES // SUM_CHUNKS, D // HALVES), BF16),
            pltpu.VMEM((D, D), BF16),
            pltpu.VMEM((1, D, D), F32),
            pltpu.VMEM((D, D), BF16),
            pltpu.VMEM((HEADS, 3, D, D), BF16),
            pltpu.VMEM((Y - 1, SUM_CHUNKS, D * HALVES // SUM_CHUNKS, D // HALVES), BF16),
            pltpu.SemaphoreType.DMA((2, 2 * Y - 1)),
            pltpu.SemaphoreType.DMA((2, 2 * Y - 1)),
            pltpu.SemaphoreType.DMA((3, SUM_CHUNKS)),
            pltpu.SemaphoreType.DMA((2, 3, SUM_CHUNKS)),
            pltpu.SemaphoreType.DMA((Y - 1, SUM_CHUNKS)),
            pltpu.SemaphoreType.DMA((3, CHUNKS, 2 + Y)),
            pltpu.SemaphoreType.DMA((HEADS, 3, CHUNKS)),
            pltpu.SemaphoreType.DMA((2,)),
            pltpu.SemaphoreType.DMA((5,)),
        ],
        compiler_params=pltpu.CompilerParams(
            collective_id=0, has_side_effects=True, vmem_limit_bytes=30 * 1024 * 1024
        ),
        name="ttt_step",
    )(*[pltpu.with_memory_space_constraint(a, pltpu.MemorySpace.HBM) for a in (keys, values, queries, rates, fast_weights)])
    anywhere = pl.BlockSpec(memory_space=pl.ANY)
    return pl.pallas_call(
        store,
        out_shape=(
            jax.ShapeDtypeStruct(out.shape, BF16),
            jax.ShapeDtypeStruct(fresh.shape, BF16),
        ),
        in_specs=[anywhere] * 2,
        out_specs=(hbm, hbm),
        scratch_shapes=[pltpu.SemaphoreType.DMA((2,))],
        compiler_params=pltpu.CompilerParams(vmem_limit_bytes=1024 * 1024),
        name="store",
    )(out, fresh)


def solution(mesh):
    chips = mesh.shape["tok"] // 2
    Y = 1
    while Y * Y * 4 <= chips and chips % (2 * Y) == 0:
        Y *= 2
    Z = chips // Y
    return jax.shard_map(
        functools.partial(body, Z, Y),
        mesh=mesh,
        in_specs=(
            P(("grp", "tok"), None),
            P(("grp", "tok"), None),
            P(("grp", "tok"), None),
            P(None, ("grp", "tok")),
            P(),
        ),
        out_specs=(P(("grp", "tok"), None), P("grp", None, None, None)),
        check_vma=False,
    )
```
